32 devices in a mesh: grp: 16 (over z, x, core), slab: 2 (over y).
Axes of the slice: x: 2, y: 2, z: 4, core: 2. Of those that a mesh axis runs over, the one named last changes fastest.
Arguments:
- ligand_grids: float32 [2, 4, 128, 128, 128], P(None, None, 'grp', 'slab'), may hold values from -6 to 6
- receptor_kernel: bfloat16 [16, 2, 2, 128, 128, 128], P('grp', None, None, 'slab'), may hold values from -3 to 3
Outputs:
- best_score: bfloat16 [16, 128, 128, 128], P('grp', None, 'slab')
The draws below stay inside these ranges and needn't reach their ends.
All inputs are finite; a program needn't handle non-finite values.
Results may differ from the reference program's by a relative error of at most 0.018.
Values may be sent and summed in bfloat16 or wider, within the bound.
A program may use at most 128 MiB of HBM per device.

```python
import math
import jax
import jax.numpy as jnp
from jax import lax

G = 128
CH = 4
PAIRS = 2
ROT = 2
REC = 16


def block_levels(own_key, dims, split, least, largest):
    factor_of = 1.0
    for position, shards_of in split:
        draws = jax.random.uniform(jax.random.fold_in(jax.random.fold_in(own_key, 6), position), (shards_of,), jnp.float32, least / len(split), largest / len(split))
        factor_of = factor_of * jnp.repeat(jnp.exp(draws), dims[position] // shards_of).reshape((-1,) + (1,) * (len(dims) - 1 - position))
    return factor_of


def scatter_about(key, dims, scale, reach, shards=(), kind=jnp.bfloat16):
    drawn = jax.random.normal(key, dims, jnp.float32) * scale
    if len(shards) > 0:
        drawn = block_levels(key, dims, shards, -0.22, 0.18) * drawn
    return jnp.clip(drawn, min=-reach, max=reach).astype(kind)


def setup_inputs(seed: int = 0) -> dict:
    splits = jax.random.split(jax.random.key(seed), 3)
    ligand_grids = scatter_about(splits[0], (ROT, CH, G, G, G), 1.0, 6.0, ((2, 16), (3, 2)), jnp.float32)
    receptor_kernel = scatter_about(splits[1], (REC, 2, PAIRS, G, G, G), 0.5, 3.0, ((0, 16), (3, 2)))
    return dict(ligand_grids=ligand_grids, receptor_kernel=receptor_kernel)


highest = lax.Precision.HIGHEST

def coefficients(length, inverse):
    positions = jnp.arange(length, dtype=jnp.int32)
    phases = positions[:, None] * positions[None, :] % length
    angles = phases.astype(jnp.float32) * (2.0 * math.pi / length)
    scaling = 1.0 / math.sqrt(length)
    cosine = jnp.cos(angles) * scaling
    sine_part = jnp.sin(angles) * scaling
    if inverse:
        sine_part = -sine_part
    upper_rows = jnp.stack([cosine, sine_part])
    lower_rows = jnp.stack([-sine_part, cosine])
    return jnp.stack([upper_rows, lower_rows])

def pack_pairs(ligand_grids):
    return jnp.stack([ligand_grids[:, 0::2], ligand_grids[:, 1::2]])

def reference(ligand_grids, receptor_kernel):
    length = ligand_grids.shape[4]
    forward = coefficients(length, False)
    forward_low = lax.optimization_barrier(forward.astype(jnp.bfloat16)).astype(jnp.float32)
    inverse_low = lax.optimization_barrier(coefficients(length, True).astype(jnp.bfloat16)).astype(jnp.float32)
    packed = pack_pairs(ligand_grids)
    along_z = jnp.einsum('pqkn,qrjnxy->prjkxy', forward, packed, precision=highest)
    partial_value = jnp.einsum('pqkn,qrjzxn->prjzxk', forward, along_z, precision=highest).astype(jnp.bfloat16)
    spectrum = jnp.einsum('pqkn,qrjznm->prjzkm', forward_low, partial_value.astype(jnp.float32), precision=highest).astype(jnp.bfloat16)
    spec_wide = spectrum.astype(jnp.float32)

    def one_receptor(kernel_one):
        kernel_wide = kernel_one.astype(jnp.float32)
        real_part = lax.optimization_barrier(jnp.sum(kernel_wide[0][None] * spec_wide[0] - kernel_wide[1][None] * spec_wide[1], axis=1))
        imag_part = lax.optimization_barrier(jnp.sum(kernel_wide[0][None] * spec_wide[1] + kernel_wide[1][None] * spec_wide[0], axis=1))
        product = jnp.stack([real_part, imag_part]).astype(jnp.bfloat16).astype(jnp.float32)
        rows_done = jnp.einsum('pqkn,qrznm->przkm', inverse_low, product, precision=highest).astype(jnp.bfloat16).astype(jnp.float32)
        planes = jnp.einsum('pqkn,qrzxn->przxk', inverse_low, rows_done, precision=highest).astype(jnp.bfloat16).astype(jnp.float32)
        scores = jnp.einsum('qkn,qrnxy->rkxy', inverse_low[0], planes, precision=highest)
        return lax.optimization_barrier(jnp.max(scores, axis=0)).astype(jnp.bfloat16)
    return lax.map(one_receptor, receptor_kernel)
```

```python
import math

import functools

import jax
import jax.numpy as jnp
import numpy as np
from jax import lax
from jax.experimental import pallas as pl
from jax.experimental.pallas import tpu as pltpu
from jax.sharding import PartitionSpec as P

highest = lax.Precision.HIGHEST


def coefficients(length, inverse):
    positions = jnp.arange(length, dtype=jnp.int32)
    phases = positions[:, None] * positions[None, :] % length
    angles = phases.astype(jnp.float32) * (2.0 * math.pi / length)
    scaling = 1.0 / math.sqrt(length)
    cosine = jnp.cos(angles) * scaling
    sine_part = jnp.sin(angles) * scaling
    if inverse:
        sine_part = -sine_part
    upper_rows = jnp.stack([cosine, sine_part])
    lower_rows = jnp.stack([-sine_part, cosine])
    return jnp.stack([upper_rows, lower_rows])


def pack_pairs(ligand_piece):
    stacked = jnp.stack([ligand_piece[:, 0::2], ligand_piece[:, 1::2]])
    return stacked.reshape((2, stacked.shape[1] * stacked.shape[2]) + stacked.shape[3:])


def body(ligand_grids, receptor_kernel):
    length = ligand_grids.shape[4]
    rotations = ligand_grids.shape[0]
    channel_pairs = ligand_grids.shape[1] // 2
    forward = coefficients(length, False)
    forward_low = forward.astype(jnp.bfloat16)
    inverse_low = coefficients(length, True).astype(jnp.bfloat16)
    packed = pack_pairs(ligand_grids)
    lines = jnp.einsum("pqkn,qrzxn->pkrzx", forward, packed, precision=highest)
    columns = lax.all_to_all(
        lines.astype(jnp.bfloat16), "grp", split_axis=1, concat_axis=3, tiled=True
    ).astype(lines.dtype)
    partial_value = jnp.einsum("pqkn,qyrnx->pyrkx", forward, columns, precision=highest).astype(
        jnp.bfloat16
    )
    pieces = jnp.einsum(
        "pqkn,qyrzn->pyrzk",
        forward_low,
        lax.all_to_all(partial_value, "slab", split_axis=3, concat_axis=4, tiled=True),
        preferred_element_type=jnp.float32,
    ).astype(jnp.bfloat16)
    collected = lax.all_gather(pieces, "grp", axis=1, tiled=True)
    spectrum = jnp.transpose(collected, (0, 2, 3, 4, 1))
    spec_split = spectrum.reshape((2, rotations, channel_pairs) + spectrum.shape[2:])
    kernel_one = receptor_kernel[0]
    kernel_real = kernel_one[0][None].astype(jnp.float32)
    kernel_imag = kernel_one[1][None].astype(jnp.float32)
    spec_real = spec_split[0].astype(jnp.float32)
    spec_imag = spec_split[1].astype(jnp.float32)
    real_part = jnp.sum(kernel_real * spec_real - kernel_imag * spec_imag, axis=1)
    imag_part = jnp.sum(kernel_real * spec_imag + kernel_imag * spec_real, axis=1)
    product = jnp.stack([real_part, imag_part]).astype(jnp.bfloat16)
    rows_done = jnp.einsum(
        "pqkn,qrznm->przkm", inverse_low, product, preferred_element_type=jnp.float32
    ).astype(jnp.bfloat16)
    planes = jnp.einsum(
        "pqkn,qrzxn->przxk", inverse_low, rows_done, preferred_element_type=jnp.float32
    ).astype(jnp.bfloat16)
    scores = jnp.einsum(
        "qkn,qrnxy->rkxy",
        inverse_low[0],
        lax.all_to_all(planes, "slab", split_axis=3, concat_axis=2, tiled=True),
        preferred_element_type=jnp.float32,
    )
    return jnp.max(scores, axis=0).astype(jnp.bfloat16)[None]


TILE = 16
SUB = 8
MOVED = 8
f32 = jnp.float32
bf16 = jnp.bfloat16


def waves(length):
    positions = np.arange(length)
    angles = (positions[:, None] * positions[None, :] % length) * (2.0 * math.pi / length)
    scaling = 1.0 / math.sqrt(length)
    cosine, sine = np.cos(angles) * scaling, np.sin(angles) * scaling
    forward = np.stack([np.stack([cosine, sine]), np.stack([-sine, cosine])])
    inverse = np.stack([np.stack([cosine, -sine]), np.stack([sine, cosine])])
    return forward, inverse


def frequencies(length, moved, own):
    half = length // 2
    base, across = own * half, (1 - own) * half
    single = [base] + [base + n for n in range(moved + 1, half - moved)]
    kept = [base + half - moved + n for n in range(moved)]
    taken = [across + moved - n for n in range(moved)]
    return single, kept, taken


def matrices(length, groups, moved):
    forward, inverse = waves(length)
    half, side = length // 2, 2 * length
    chips = groups // 2
    orders, lasting = [], []
    for own in range(2):
        single, kept, taken = frequencies(length, moved, own)
        orders.append(single + [k for both in zip(kept, taken) for k in both])
        lasting.append(single + kept)
    fz, ix, mz = [], [], []
    for own in range(2):
        order = np.array(orders[own] + orders[1 - own])
        fz.append(forward[:, :, order].transpose(0, 2, 1, 3).reshape(side, side))
        order = (np.arange(length) + own * half) % length
        ix.append(inverse[:, :, order].transpose(0, 2, 1, 3).reshape(side, side))
        order = np.array(lasting[own] + lasting[1 - own])
        lines = inverse[0][:, :, order].reshape(2, length, len(order) // SUB, SUB)
        mz.append(lines.transpose(1, 2, 0, 3).reshape(length, 2 * len(order)))
    cells = forward.reshape(2, 2, length, 2, chips, half // chips)
    fx = cells.transpose(0, 2, 4, 3, 1, 5).reshape(side, side)
    fy = forward.transpose(1, 3, 0, 2).reshape(side, side)
    iy = inverse.transpose(1, 3, 0, 2).reshape(side, side)
    return [jnp.asarray(np.stack(m) if isinstance(m, list) else m).astype(bf16) for m in (fz, fy, fx, ix, iy, mz)]


def dot(a, b):
    return jnp.dot(a, b, preferred_element_type=f32)


def front_kernel(
    moved, groups, lig_ref, rec_ref, fy_ref, fz_ref, near_ref, swap_ref, give_ref,
    blocks, lines, along, hold, line_out, line_in, own_sem, give_out, give_in,
):
    me = lax.axis_index("grp")
    slab = lax.axis_index("slab")
    core = lax.rem(me, 2)
    chip = lax.div(me, 2)
    rotations, channels, depth, width, length = lig_ref.shape
    pairs = channels // 2
    chips = groups // 2
    block = width // chips
    rows = depth * block
    half = length // 2
    MESH = pl.DeviceIdType.MESH
    across = {"grp": me, "slab": 1 - slab}
    barrier = pltpu.get_barrier_semaphore()
    pl.semaphore_signal(barrier, inc=1, device_id=across, device_id_type=MESH)

    @pl.loop(1, groups)
    def _(o):
        to = {"grp": lax.rem(me + o, groups), "slab": slab}
        pl.semaphore_signal(barrier, inc=1, device_id=to, device_id_type=MESH)

    @pl.loop(0, chips)
    def _(b):
        for r in range(rotations):
            for j in range(pairs):
                for q in range(2):
                    piece = lig_ref[r, 2 * j + q, :, pl.ds(pl.multiple_of(b * block, block), block), :]
                    blocks[b, r, j, q] = piece.reshape(rows, length).astype(bf16)

    pl.semaphore_wait(barrier, groups)

    def give(p, j):
        return pltpu.make_async_remote_copy(
            src_ref=rec_ref.at[p, j, pl.ds(1, moved)], dst_ref=give_ref.at[p, j],
            send_sem=give_out.at[p, j], recv_sem=give_in.at[p, j],
            device_id=across, device_id_type=MESH,
        )

    def line(o, j):
        to = lax.rem(me + o, groups)
        return pltpu.make_async_remote_copy(
            src_ref=blocks.at[lax.div(to, 2), lax.rem(to, 2), j], dst_ref=lines.at[j, me],
            send_sem=line_out.at[j, o], recv_sem=line_in.at[j, o],
            device_id={"grp": to, "slab": slab}, device_id_type=MESH,
        )

    def stay(j):
        return pltpu.make_async_copy(blocks.at[chip, core, j], lines.at[j, me], own_sem.at[j])

    for j in range(pairs):
        @pl.loop(1, groups)
        def _(o):
            line(o, j).start()

        stay(j).start()
    if moved:
        for p in range(2):
            for j in range(pairs):
                give(p, j).start()

    def along_y(j, g):
        plane = dot(jnp.concatenate([lines[j, g, 0], lines[j, g, 1]], 1), fy_ref[...])
        for p in range(2):
            at = pl.ds(pl.multiple_of(g * rows, rows), rows)
            along[p, at, :] = plane[:, p * length : (p + 1) * length]

    for j in range(pairs):
        stay(j).wait()
        along_y(j, me)

        @pl.loop(1, groups)
        def _(o):
            line(o, j).wait_recv()
            along_y(j, lax.rem(me + groups - o, groups))

        @pl.loop(0, block)
        def _(x):
            parts = [along[p, pl.ds(x, length, stride=block), :].astype(bf16) for p in range(2)]
            found = dot(fz_ref[slab], jnp.concatenate(parts, 0))
            for p in range(2):
                at = pl.ds(pl.multiple_of((p * block + x) * length, length), length)
                hold[at, :] = found[p * length : (p + 1) * length, :]

        @pl.loop(0, half, unroll=4)
        def _(k):
            near_ref[k, j] = hold[pl.ds(k, 2 * block, stride=length), :].astype(bf16)
            swap_ref[k, j] = hold[pl.ds(half + k, 2 * block, stride=length), :].astype(bf16)

    for j in range(pairs):
        @pl.loop(1, groups)
        def _(o):
            line(o, j).wait_send()

    if moved:
        for p in range(2):
            for j in range(pairs):
                give(p, j).wait()


def score_kernel(
    rotations, groups, length, chunks, moved, fx_ref, ix_ref, iy_ref, mz_ref, rec_ref, give_ref, near_ref, swap_ref, out_ref,
    mine_ref, far_ref, held, rec, send, hold, rec_sem, near_sem, swap_out, swap_in, ring_out, ring_in, pair_out, pair_in, slab_out, slab_in,
):
    me = lax.axis_index("grp")
    slab = lax.axis_index("slab")
    core = lax.rem(me, 2)
    half = length // 2
    single = (half - 2 * moved) // SUB
    lasting = single + moved // SUB
    height = groups // 4
    around = groups // 2
    row = me // 4
    column = lax.rem(me // 2, 2)
    spot = jnp.where(column == 0, row, around - 1 - row)

    def device(at, which):
        at = lax.rem(at + around, around)
        return jnp.where(at < height, at * 4, (around - 1 - at) * 4 + 2) + which

    beside = (device(spot + 1, core), device(spot - 1, core))
    partner = device(spot, 1 - core)

    def place(to):
        return {"grp": to, "slab": slab}

    across = {"grp": me, "slab": 1 - slab}
    MESH = pl.DeviceIdType.MESH
    rest = half - 1 - moved
    loads = [
        pltpu.make_async_copy(from_ref, rec.at[:, :, pl.ds(at, many)], rec_sem.at[n])
        for n, (from_ref, at, many) in enumerate(
            [
                (rec_ref.at[:, :, pl.ds(0, 1)], 0, 1),
                (rec_ref.at[:, :, pl.ds(moved + 1, rest)], moved + 1, rest),
            ]
            + [(give_ref, 1, moved)] * (moved > 0)
        )
    ]
    place_own = pltpu.make_async_copy(near_ref, held.at[me, slab], near_sem)
    place_own.start()
    for load in loads:
        load.start()
    barrier = pltpu.get_barrier_semaphore()
    for to in (place(beside[0]), place(beside[1]), place(partner), across):
        pl.semaphore_signal(barrier, inc=1, device_id=to, device_id_type=MESH)
    pl.semaphore_wait(barrier, 4)

    def swap(c):
        at = pl.ds(c * SUB, SUB)
        return pltpu.make_async_remote_copy(
            src_ref=swap_ref.at[at], dst_ref=held.at[me, slab, at],
            send_sem=swap_out.at[c], recv_sem=swap_in.at[c],
            device_id=across, device_id_type=MESH,
        )

    @pl.loop(0, chunks)
    def _(c):
        swap(c).start()

    def join(c):
        swap(c).wait_recv()

    def origin(d, t):
        return spot - t if d == 0 else spot + t

    def part(slot, c):
        return held.at[slot, :, pl.ds(c * SUB, SUB)]

    def ring(d, c, t, slot):
        return pltpu.make_async_remote_copy(
            src_ref=part(slot, c), dst_ref=part(slot, c),
            send_sem=ring_out.at[d, c, t], recv_sem=ring_in.at[d, c, t],
            device_id=place(beside[d]), device_id_type=MESH,
        )

    def ring_send(d, c, t):
        ring(d, c, t, device(origin(d, t), core)).start()

    def ring_wait(d, c, t):
        ring(d, c, t, device(origin(d, t + 1), core)).wait_recv()

    def pair(d, c, t, which):
        slot = device(origin(d, t), which)
        return pltpu.make_async_remote_copy(
            src_ref=part(slot, c), dst_ref=part(slot, c),
            send_sem=pair_out.at[d, c, t], recv_sem=pair_in.at[d, c, t],
            device_id=place(partner), device_id_type=MESH,
        )

    def slab_copy(c, q):
        at = pl.ds(pl.multiple_of(q * TILE, TILE), TILE)
        return pltpu.make_async_remote_copy(
            src_ref=send.at[c, :, at], dst_ref=far_ref.at[c, :, at],
            send_sem=slab_out.at[c, q], recv_sem=slab_in.at[c, q],
            device_id=across, device_id_type=MESH,
        )

    far_step = around // 2 - 1

    def for_far(c, act):
        for d in range(2):
            @pl.when(lax.rem(c, 2) == d)
            def _():
                act(d)

    def arrived(c, t):
        for d in range(2):
            ring_wait(d, c, t)
            if t + 1 < far_step:
                ring_send(d, c, t + 1)
            pair(d, c, t + 1, core).start()

    rows = rotations * length
    chips = groups // 2

    def plane(z, slot):
        kr = [rec[0, j, slot].astype(f32) for j in range(2)]
        ki = [rec[1, j, slot].astype(f32) for j in range(2)]
        real, imag = [], []
        for r in range(rotations):
            cols = [
                jnp.concatenate([held[2 * b + r, s, z, j] for b in range(chips) for s in range(2)], 0)
                for j in range(2)
            ]
            spec = dot(fx_ref[...], jnp.concatenate(cols, 1))
            sr = [spec[:length, j * length : (j + 1) * length] for j in range(2)]
            si = [spec[length:, j * length : (j + 1) * length] for j in range(2)]
            real.append(kr[0] * sr[0] - ki[0] * si[0] + (kr[1] * sr[1] - ki[1] * si[1]))
            imag.append(kr[0] * si[0] + ki[0] * sr[0] + (kr[1] * si[1] + ki[1] * sr[1]))
        product = jnp.concatenate(
            [jnp.concatenate(real, 1).astype(bf16), jnp.concatenate(imag, 1).astype(bf16)], 0
        )
        done = dot(ix_ref[slab], product).astype(bf16)
        flat = []
        for r in range(rotations):
            at = slice(r * length, (r + 1) * length)
            flat.append(jnp.concatenate([done[:length, at], done[length:, at]], 1))
        return dot(jnp.concatenate(flat, 0), iy_ref[...])

    def keep(k, parts):
        for p in range(2):
            hold[p, pl.ds(pl.multiple_of(k * rows, rows), rows), :] = parts[p]

    def alone(c, first):
        @pl.loop(first, first + SUB // 2, unroll=2)
        def _(k):
            z = c * SUB + k
            both = plane(z, jnp.where(z == 0, 0, z + moved))
            keep(k, [both[:, :length], both[:, length:]])

    def mirrored(c, first):
        @pl.loop(0, SUB // 4)
        def _(q):
            z = c * SUB + first + 2 * q
            n = lax.div(z - single * SUB, 2)
            one = plane(z, half - moved + n)
            two = plane(z + 1, moved - n)
            keep(lax.rem(n, SUB), [one[:, :length] + two[:, :length], one[:, length:] - two[:, length:]])

    def compute(c, first):
        @pl.when(c < single)
        def _():
            alone(c, first)

        if moved:
            @pl.when(c >= single)
            def _():
                mirrored(c, first)

    def collect(c, ref, first):
        @pl.loop(0, half, unroll=4)
        def _(x):
            for r in range(rotations):
                at = pl.ds(r * length + first + x, SUB, stride=rows)
                ref[c, r, x] = jnp.concatenate([hold[0, at, :], hold[1, at, :]], 0).astype(bf16)

    def open_chunk(c):
        for d in range(2):
            ring_send(d, c, 0)
        pair(0, c, 0, core).start()

    place_own.wait()
    join(0)
    open_chunk(0)

    @pl.loop(0, chunks + 2)
    def _(i):
        c1, c2 = i - 1, i - 2

        @pl.when((c1 >= 0) & (c1 < chunks))
        def _():
            arrived(c1, 1)

        @pl.when(i + 1 < chunks)
        def _():
            join(i + 1)

        @pl.when(i == 2)
        def _():
            for load in loads:
                load.wait()

        @pl.when(c2 >= 0)
        def _():
            def act(d):
                ring_wait(d, c2, far_step)
                pair(d, c2, far_step + 1, core).start()

            for_far(c2, act)
            pair(0, c2, 0, 1 - core).wait_recv()
            for t in range(1, far_step + 1):
                for d in range(2):
                    pair(d, c2, t, 1 - core).wait_recv()
            for_far(c2, lambda d: pair(d, c2, far_step + 1, 1 - core).wait_recv())
            compute(c2, 0)

        @pl.when(i < chunks)
        def _():
            arrived(i, 0)

        @pl.when((c1 >= 0) & (c1 < chunks))
        def _():
            arrived(c1, 2)
            for_far(c1, lambda d: ring_send(d, c1, far_step))

        @pl.when(i + 1 < chunks)
        def _():
            open_chunk(i + 1)

        @pl.when(c2 >= 0)
        def _():
            compute(c2, SUB // 2)
            over = c2 - single

            @pl.when((over < 0) | (lax.rem(jnp.maximum(over, 0), 2) == 1))
            def _():
                c = jnp.where(over < 0, c2, single + lax.div(jnp.maximum(over, 0), 2))
                collect(c, send, half)
                collect(c, mine_ref, 0)
                for q in range(half // TILE):
                    slab_copy(c, q).start()

    @pl.loop(0, chunks)
    def _(c):
        for t in range(far_step):
            for d in range(2):
                ring(d, c, t, device(origin(d, t), core)).wait_send()
                pair(d, c, t + 1, core).wait_send()
        pair(0, c, 0, core).wait_send()

        def act(d):
            ring(d, c, far_step, device(origin(d, far_step), core)).wait_send()
            pair(d, c, far_step + 1, core).wait_send()

        for_far(c, act)
        swap(c).wait_send()

    @pl.loop(0, half // TILE)
    def _(q):
        @pl.loop(0, lasting)
        def _(c):
            slab_copy(c, q).wait_send()
            slab_copy(c, q).wait_recv()

        @pl.loop(0, TILE, unroll=2)
        def _(x):
            cols = []
            for r in range(rotations):
                tiles = [
                    ref[t, r, q * TILE + x] for ref in (mine_ref, far_ref) for t in range(lasting)
                ]
                cols.append(jnp.concatenate(tiles, 0))
            scores = dot(mz_ref[slab], jnp.concatenate(cols, 1))
            best = scores[:, :length]
            for r in range(1, rotations):
                best = jnp.maximum(best, scores[:, r * length : (r + 1) * length])
            hold[0, pl.ds(x * length, length), :] = best

        @pl.loop(0, length, unroll=4)
        def _(z):
            at = pl.ds(pl.multiple_of(q * TILE, TILE), TILE)
            out_ref[z, at, :] = hold[0, pl.ds(z, TILE, stride=length), :].astype(bf16)


def quick_body(groups, ligand_grids, receptor_kernel):
    rotations, channels, depth, width, length = ligand_grids.shape
    pairs = channels // 2
    half = length // 2
    chips = groups // 2
    block = width // chips
    rows = depth * block
    moved = MOVED
    fz, fy, fx, ix, iy, mz = matrices(length, groups, moved)
    whole = pl.BlockSpec(memory_space=pltpu.VMEM)
    away = pl.BlockSpec(memory_space=pl.ANY)
    dma = pltpu.SemaphoreType.DMA
    rec = receptor_kernel[0]

    shape = jax.ShapeDtypeStruct((half, pairs, 2 * block, length), bf16)
    given = jax.ShapeDtypeStruct((2, pairs, moved, length, length), bf16)
    near, other, give = pl.pallas_call(
        functools.partial(front_kernel, moved, groups),
        out_shape=[shape, shape, given],
        in_specs=[whole, away, whole, whole],
        out_specs=[whole, whole, away],
        scratch_shapes=[
            pltpu.VMEM((chips, rotations, pairs, 2, rows, length), bf16),
            pltpu.VMEM((pairs, groups, 2, rows, length), bf16),
            pltpu.VMEM((2, block * length, length), f32),
            pltpu.VMEM((2 * block * length, length), f32),
            dma((pairs, groups)),
            dma((pairs, groups)),
            dma((pairs,)),
            dma((2, pairs)),
            dma((2, pairs)),
        ],
        compiler_params=pltpu.CompilerParams(
            collective_id=1, has_side_effects=True, vmem_limit_bytes=24 * 2**20
        ),
    )(ligand_grids, rec, fy, fz)

    chunks = half // SUB
    hops = groups // 4
    lasting = chunks - moved // SUB
    part = (lasting, rotations, half, TILE, length)
    best = pl.pallas_call(
        functools.partial(score_kernel, rotations, groups, length, chunks, moved),
        out_shape=jax.ShapeDtypeStruct((length, half, length), bf16),
        in_specs=[whole] * 4 + [away] * 4,
        out_specs=whole,
        scratch_shapes=[
            pltpu.VMEM(part, bf16),
            pltpu.VMEM(part, bf16),
            pltpu.VMEM((groups, 2, half, pairs, TILE, length), bf16),
            pltpu.VMEM(rec.shape, bf16),
            pltpu.VMEM(part, bf16),
            pltpu.VMEM((2, SUB * rotations * length, length), f32),
            dma((3,)),
            dma,
            dma((chunks,)),
            dma((chunks,)),
            dma((2, chunks, hops)),
            dma((2, chunks, hops)),
            dma((2, chunks, hops + 1)),
            dma((2, chunks, hops + 1)),
            dma((lasting, half // TILE)),
            dma((lasting, half // TILE)),
        ],
        compiler_params=pltpu.CompilerParams(
            collective_id=0, has_side_effects=True, vmem_limit_bytes=60 * 2**20
        ),
    )(fx, ix, iy, mz, rec, give, near, other)

    return best[None]


def choose(groups, slabs, ligand_grids, receptor_kernel):
    rotations, channels, depth, width, length = ligand_grids.shape
    fits = (
        slabs == 2
        and channels == 4
        and rotations == 2
        and depth == SUB
        and depth * groups == length
        and 2 * width == length
        and width // (groups // 2) == SUB
        and length % 128 == 0
        and (length // 2) % SUB == 0
        and groups == 4 * 4
        and (length // 2) % TILE == 0
    )
    if fits:
        return quick_body(groups, ligand_grids, receptor_kernel)
    return body(ligand_grids, receptor_kernel)


def solution(mesh):
    return jax.shard_map(
        functools.partial(choose, mesh.shape["grp"], mesh.shape["slab"]),
        mesh=mesh,
        in_specs=(P(None, None, "grp", "slab", None), P("grp", None, None, "slab", None, None)),
        out_specs=P("grp", None, "slab", None),
        check_vma=False,
    )
```

```python
import math

import functools

import jax
import jax.numpy as jnp
import numpy as np
from jax import lax
from jax.experimental import pallas as pl
from jax.experimental.pallas import tpu as pltpu
from jax.sharding import PartitionSpec as P

highest = lax.Precision.HIGHEST


def coefficients(length, inverse):
    positions = jnp.arange(length, dtype=jnp.int32)
    phases = positions[:, None] * positions[None, :] % length
    angles = phases.astype(jnp.float32) * (2.0 * math.pi / length)
    scaling = 1.0 / math.sqrt(length)
    cosine = jnp.cos(angles) * scaling
    sine_part = jnp.sin(angles) * scaling
    if inverse:
        sine_part = -sine_part
    upper_rows = jnp.stack([cosine, sine_part])
    lower_rows = jnp.stack([-sine_part, cosine])
    return jnp.stack([upper_rows, lower_rows])


def pack_pairs(ligand_piece):
    stacked = jnp.stack([ligand_piece[:, 0::2], ligand_piece[:, 1::2]])
    return stacked.reshape((2, stacked.shape[1] * stacked.shape[2]) + stacked.shape[3:])


def body(ligand_grids, receptor_kernel):
    length = ligand_grids.shape[4]
    rotations = ligand_grids.shape[0]
    channel_pairs = ligand_grids.shape[1] // 2
    forward = coefficients(length, False)
    forward_low = forward.astype(jnp.bfloat16)
    inverse_low = coefficients(length, True).astype(jnp.bfloat16)
    packed = pack_pairs(ligand_grids)
    lines = jnp.einsum("pqkn,qrzxn->pkrzx", forward, packed, precision=highest)
    columns = lax.all_to_all(
        lines.astype(jnp.bfloat16), "grp", split_axis=1, concat_axis=3, tiled=True
    ).astype(lines.dtype)
    partial_value = jnp.einsum("pqkn,qyrnx->pyrkx", forward, columns, precision=highest).astype(
        jnp.bfloat16
    )
    pieces = jnp.einsum(
        "pqkn,qyrzn->pyrzk",
        forward_low,
        lax.all_to_all(partial_value, "slab", split_axis=3, concat_axis=4, tiled=True),
        preferred_element_type=jnp.float32,
    ).astype(jnp.bfloat16)
    collected = lax.all_gather(pieces, "grp", axis=1, tiled=True)
    spectrum = jnp.transpose(collected, (0, 2, 3, 4, 1))
    spec_split = spectrum.reshape((2, rotations, channel_pairs) + spectrum.shape[2:])
    kernel_one = receptor_kernel[0]
    kernel_real = kernel_one[0][None].astype(jnp.float32)
    kernel_imag = kernel_one[1][None].astype(jnp.float32)
    spec_real = spec_split[0].astype(jnp.float32)
    spec_imag = spec_split[1].astype(jnp.float32)
    real_part = jnp.sum(kernel_real * spec_real - kernel_imag * spec_imag, axis=1)
    imag_part = jnp.sum(kernel_real * spec_imag + kernel_imag * spec_real, axis=1)
    product = jnp.stack([real_part, imag_part]).astype(jnp.bfloat16)
    rows_done = jnp.einsum(
        "pqkn,qrznm->przkm", inverse_low, product, preferred_element_type=jnp.float32
    ).astype(jnp.bfloat16)
    planes = jnp.einsum(
        "pqkn,qrzxn->przxk", inverse_low, rows_done, preferred_element_type=jnp.float32
    ).astype(jnp.bfloat16)
    scores = jnp.einsum(
        "qkn,qrnxy->rkxy",
        inverse_low[0],
        lax.all_to_all(planes, "slab", split_axis=3, concat_axis=2, tiled=True),
        preferred_element_type=jnp.float32,
    )
    return jnp.max(scores, axis=0).astype(jnp.bfloat16)[None]


TILE = 16
SUB = 8
MOVED = 8
f32 = jnp.float32
bf16 = jnp.bfloat16


def waves(length):
    positions = np.arange(length)
    angles = (positions[:, None] * positions[None, :] % length) * (2.0 * math.pi / length)
    scaling = 1.0 / math.sqrt(length)
    cosine, sine = np.cos(angles) * scaling, np.sin(angles) * scaling
    forward = np.stack([np.stack([cosine, sine]), np.stack([-sine, cosine])])
    inverse = np.stack([np.stack([cosine, -sine]), np.stack([sine, cosine])])
    return forward, inverse


def frequencies(length, moved, own):
    half = length // 2
    base, across = own * half, (1 - own) * half
    single = [base] + [base + n for n in range(moved + 1, half - moved)]
    kept = [base + half - moved + n for n in range(moved)]
    taken = [across + moved - n for n in range(moved)]
    return single, kept, taken


def matrices(length, groups, moved):
    forward, inverse = waves(length)
    half, side = length // 2, 2 * length
    chips = groups // 2
    orders, lasting = [], []
    for own in range(2):
        single, kept, taken = frequencies(length, moved, own)
        orders.append(single + [k for both in zip(kept, taken) for k in both])
        lasting.append(single + kept)
    fz, ix, mz = [], [], []
    for own in range(2):
        order = np.array(orders[own] + orders[1 - own])
        fz.append(forward[:, :, order].transpose(0, 2, 1, 3).reshape(side, side))
        order = (np.arange(length) + own * half) % length
        ix.append(inverse[:, :, order].transpose(0, 2, 1, 3).reshape(side, side))
        order = np.array(lasting[own] + lasting[1 - own])
        lines = inverse[0][:, :, order].reshape(2, length, len(order) // SUB, SUB)
        mz.append(lines.transpose(1, 2, 0, 3).reshape(length, 2 * len(order)))
    cells = forward.reshape(2, 2, length, 2, chips, half // chips)
    fx = cells.transpose(0, 2, 4, 3, 1, 5).reshape(side, side)
    fy = forward.transpose(1, 3, 0, 2).reshape(side, side)
    iy = inverse.transpose(1, 3, 0, 2).reshape(side, side)
    return [jnp.asarray(np.stack(m) if isinstance(m, list) else m).astype(bf16) for m in (fz, fy, fx, ix, iy, mz)]


def dot(a, b):
    return jnp.dot(a, b, preferred_element_type=f32)


def dock_kernel(
    groups, moved, fz_ref, fy_ref, fx_ref, ix_ref, iy_ref, mz_ref, lig_ref, rec_ref, out_ref,
    lig, blocks, lines, along, other, held, rec, mine, far, send, hold,
    lig_sem, rec_sem, own_sem, line_out, line_in, give_out, give_in,
    swap_out, swap_in, ring_out, ring_in, pair_out, pair_in, slab_out, slab_in,
):
    me = lax.axis_index("grp")
    slab = lax.axis_index("slab")
    core = lax.rem(me, 2)
    chip = lax.div(me, 2)
    rotations, channels, depth, width, length = lig_ref.shape
    pairs = channels // 2
    chips = groups // 2
    block = width // chips
    lot = depth * block
    half = length // 2
    chunks = half // SUB
    single = (half - 2 * moved) // SUB
    lasting = single + moved // SUB
    rows = rotations * length
    height = groups // 4
    around = groups // 2
    row = lax.div(me, 4)
    column = lax.rem(chip, 2)
    spot = jnp.where(column == 0, row, around - 1 - row)
    far_step = around // 2 - 1
    MESH = pl.DeviceIdType.MESH

    def device(at, which):
        at = lax.rem(at + around, around)
        return jnp.where(at < height, at * 4, (around - 1 - at) * 4 + 2) + which

    def place(to):
        return {"grp": to, "slab": slab}

    def turned(by):
        return lax.rem(me + groups + by, groups)

    beside = (device(spot + 1, core), device(spot - 1, core))
    partner = device(spot, 1 - core)
    across = {"grp": me, "slab": 1 - slab}

    lig_loads = [
        pltpu.make_async_copy(lig_ref.at[:, pl.ds(2 * j, 2)], lig.at[:, pl.ds(2 * j, 2)], lig_sem.at[j])
        for j in range(pairs)
    ]
    rest = half - 1 - moved
    rec_loads = [
        pltpu.make_async_copy(
            rec_ref.at[:, :, pl.ds(at, many)], rec.at[:, :, pl.ds(at, many)], rec_sem.at[n]
        )
        for n, (at, many) in enumerate([(0, 1), (moved + 1, rest)])
    ]
    for load in lig_loads:
        load.start()
    for load in rec_loads:
        load.start()

    barrier = pltpu.get_barrier_semaphore()
    pl.semaphore_signal(barrier, inc=1, device_id=across, device_id_type=MESH)

    @pl.loop(1, groups)
    def _(o):
        pl.semaphore_signal(barrier, inc=1, device_id=place(turned(o)), device_id_type=MESH)

    def give(p, j):
        at = pl.ds(1, moved)
        return pltpu.make_async_remote_copy(
            src_ref=rec_ref.at[p, j, at], dst_ref=rec.at[p, j, at],
            send_sem=give_out.at[p, j], recv_sem=give_in.at[p, j],
            device_id=across, device_id_type=MESH,
        )

    gives = [give(p, j) for p in range(2) for j in range(pairs)] if moved else []

    def line(o, j):
        to = turned(o)
        return pltpu.make_async_remote_copy(
            src_ref=blocks.at[lax.div(to, 2), lax.rem(to, 2), j], dst_ref=lines.at[j, me],
            send_sem=line_out.at[j, o], recv_sem=line_in.at[j, o],
            device_id=place(to), device_id_type=MESH,
        )

    def stay(j):
        return pltpu.make_async_copy(blocks.at[chip, core, j], lines.at[j, me], own_sem.at[j])

    for j in range(pairs):
        lig_loads[j].wait()

        @pl.loop(0, chips)
        def _(b):
            for r in range(rotations):
                for q in range(2):
                    piece = lig[r, 2 * j + q, :, pl.ds(pl.multiple_of(b * block, block), block), :]
                    blocks[b, r, j, q] = piece.reshape(lot, length).astype(bf16)

        if j == 0:
            pl.semaphore_wait(barrier, groups)

        @pl.loop(1, groups)
        def _(o):
            line(o, j).start()

        stay(j).start()
    for copy in gives:
        copy.start()

    def along_y(j, g):
        plane = dot(jnp.concatenate([lines[j, g, 0], lines[j, g, 1]], 1), fy_ref[...])
        for p in range(2):
            at = pl.ds(pl.multiple_of(g * lot, lot), lot)
            along[p, at, :] = plane[:, p * length : (p + 1) * length]

    def along_z():
        @pl.loop(0, block)
        def _(x):
            parts = [along[p, pl.ds(x, length, stride=block), :].astype(bf16) for p in range(2)]
            found = dot(fz_ref[slab], jnp.concatenate(parts, 0))
            for p in range(2):
                at = pl.ds(pl.multiple_of((p * block + x) * length, length), length)
                hold[0, at, :] = found[p * length : (p + 1) * length, :]

    def swap(c):
        at = pl.ds(c * SUB, SUB)
        return pltpu.make_async_remote_copy(
            src_ref=other.at[at], dst_ref=held.at[me, slab, at],
            send_sem=swap_out.at[c], recv_sem=swap_in.at[c],
            device_id=across, device_id_type=MESH,
        )

    for j in range(pairs):
        stay(j).wait()
        along_y(j, me)

        @pl.loop(1, groups)
        def _(o):
            line(o, j).wait_recv()
            along_y(j, turned(-o))

        along_z()

        @pl.loop(0, chunks)
        def _(c):
            @pl.loop(0, SUB, unroll=4)
            def _(n):
                k = c * SUB + n
                other[k, j] = hold[0, pl.ds(half + k, 2 * block, stride=length), :].astype(bf16)
                held[me, slab, k, j] = hold[0, pl.ds(k, 2 * block, stride=length), :].astype(bf16)

            if j == pairs - 1:
                swap(c).start()

    def origin(d, t):
        return spot - t if d == 0 else spot + t

    def part(slot, c, d, t):
        if t <= far_step:
            return held.at[slot, :, pl.ds(c * SUB, SUB)]
        return held.at[slot, :, pl.ds(c * SUB + d * (SUB // 2), SUB // 2)]

    def ring(d, c, t, slot):
        return pltpu.make_async_remote_copy(
            src_ref=part(slot, c, d, t + 1), dst_ref=part(slot, c, d, t + 1),
            send_sem=ring_out.at[d, c, t], recv_sem=ring_in.at[d, c, t],
            device_id=place(beside[d]), device_id_type=MESH,
        )

    def ring_send(d, c, t):
        ring(d, c, t, device(origin(d, t), core)).start()

    def ring_wait(d, c, t):
        ring(d, c, t, device(origin(d, t + 1), core)).wait_recv()

    def pair(d, c, t, which):
        slot = device(origin(d, t), which)
        return pltpu.make_async_remote_copy(
            src_ref=part(slot, c, d, t), dst_ref=part(slot, c, d, t),
            send_sem=pair_out.at[d, c, t], recv_sem=pair_in.at[d, c, t],
            device_id=place(partner), device_id_type=MESH,
        )

    def slab_copy(c, q):
        at = pl.ds(pl.multiple_of(q * TILE, TILE), TILE)
        return pltpu.make_async_remote_copy(
            src_ref=send.at[c, :, at], dst_ref=far.at[c, :, at],
            send_sem=slab_out.at[c, q], recv_sem=slab_in.at[c, q],
            device_id=across, device_id_type=MESH,
        )

    def open_chunk(c):
        swap(c).wait_recv()
        for d in range(2):
            ring_send(d, c, 0)
        pair(0, c, 0, core).start()

    def arrived(c, t):
        for d in range(2):
            ring_wait(d, c, t)
            if t < far_step:
                ring_send(d, c, t + 1)
            pair(d, c, t + 1, core).start()

    def plane(z, slot):
        kr = [rec[0, j, slot].astype(f32) for j in range(pairs)]
        ki = [rec[1, j, slot].astype(f32) for j in range(pairs)]
        real, imag = [], []
        for r in range(rotations):
            cols = [
                jnp.concatenate([held[2 * b + r, s, z, j] for b in range(chips) for s in range(2)], 0)
                for j in range(pairs)
            ]
            spec = dot(fx_ref[...], jnp.concatenate(cols, 1))
            sr = [spec[:length, j * length : (j + 1) * length] for j in range(pairs)]
            si = [spec[length:, j * length : (j + 1) * length] for j in range(pairs)]
            real.append(kr[0] * sr[0] - ki[0] * si[0] + (kr[1] * sr[1] - ki[1] * si[1]))
            imag.append(kr[0] * si[0] + ki[0] * sr[0] + (kr[1] * si[1] + ki[1] * sr[1]))
        product = jnp.concatenate(
            [jnp.concatenate(real, 1).astype(bf16), jnp.concatenate(imag, 1).astype(bf16)], 0
        )
        done = dot(ix_ref[slab], product).astype(bf16)
        flat = []
        for r in range(rotations):
            at = slice(r * length, (r + 1) * length)
            flat.append(jnp.concatenate([done[:length, at], done[length:, at]], 1))
        return dot(jnp.concatenate(flat, 0), iy_ref[...])

    def keep(k, parts):
        for p in range(2):
            hold[p, pl.ds(pl.multiple_of(k * rows, rows), rows), :] = parts[p]

    def alone(c, first):
        @pl.loop(first, first + SUB // 2, unroll=2)
        def _(k):
            z = c * SUB + k
            both = plane(z, jnp.where(z == 0, 0, z + moved))
            keep(k, [both[:, :length], both[:, length:]])

    def mirrored(c, first):
        @pl.loop(0, SUB // 4)
        def _(q):
            z = c * SUB + first + 2 * q
            n = lax.div(z - single * SUB, 2)
            one = plane(z, half - moved + n)
            two = plane(z + 1, moved - n)
            keep(lax.rem(n, SUB), [one[:, :length] + two[:, :length], one[:, length:] - two[:, length:]])

    def compute(c, first):
        @pl.when(c < single)
        def _():
            alone(c, first)

        if moved:
            @pl.when(c >= single)
            def _():
                mirrored(c, first)

    def collect(c, ref, first):
        @pl.loop(0, half, unroll=4)
        def _(x):
            for r in range(rotations):
                at = pl.ds(r * length + first + x, SUB, stride=rows)
                ref[c, r, x] = jnp.concatenate([hold[0, at, :], hold[1, at, :]], 0).astype(bf16)

    open_chunk(0)

    @pl.loop(0, chunks + 2)
    def _(i):
        c1, c2 = i - 1, i - 2

        @pl.when((c1 >= 0) & (c1 < chunks))
        def _():
            arrived(c1, 1)

        @pl.when(i == 2)
        def _():
            for load in rec_loads:
                load.wait()
            for copy in gives:
                copy.wait()

        @pl.when(c2 >= 0)
        def _():
            arrived(c2, far_step)
            pair(0, c2, 0, 1 - core).wait_recv()
            for t in range(1, far_step + 2):
                for d in range(2):
                    pair(d, c2, t, 1 - core).wait_recv()
            compute(c2, 0)

        @pl.when(i < chunks)
        def _():
            arrived(i, 0)

        @pl.when((c1 >= 0) & (c1 < chunks))
        def _():
            arrived(c1, 2)

        @pl.when(i + 1 < chunks)
        def _():
            open_chunk(i + 1)

        @pl.when(c2 >= 0)
        def _():
            compute(c2, SUB // 2)
            over = c2 - single

            @pl.when((over < 0) | (lax.rem(jnp.maximum(over, 0), 2) == 1))
            def _():
                c = jnp.where(over < 0, c2, single + lax.div(jnp.maximum(over, 0), 2))
                collect(c, send, half)
                collect(c, mine, 0)
                for q in range(half // TILE):
                    slab_copy(c, q).start()

    for j in range(pairs):
        @pl.loop(1, groups)
        def _(o):
            line(o, j).wait_send()

    @pl.loop(0, chunks)
    def _(c):
        for t in range(far_step + 1):
            for d in range(2):
                ring(d, c, t, device(origin(d, t), core)).wait_send()
                pair(d, c, t + 1, core).wait_send()
        pair(0, c, 0, core).wait_send()
        swap(c).wait_send()

    @pl.loop(0, half // TILE)
    def _(q):
        @pl.loop(0, lasting)
        def _(c):
            slab_copy(c, q).wait_send()
            slab_copy(c, q).wait_recv()

        @pl.loop(0, TILE, unroll=2)
        def _(x):
            cols = []
            for r in range(rotations):
                tiles = [ref[t, r, q * TILE + x] for ref in (mine, far) for t in range(lasting)]
                cols.append(jnp.concatenate(tiles, 0))
            scores = dot(mz_ref[slab], jnp.concatenate(cols, 1))
            best = scores[:, :length]
            for r in range(1, rotations):
                best = jnp.maximum(best, scores[:, r * length : (r + 1) * length])
            hold[0, pl.ds(x * length, length), :] = best

        @pl.loop(0, length, unroll=4)
        def _(z):
            at = pl.ds(pl.multiple_of(q * TILE, TILE), TILE)
            out_ref[z, at, :] = hold[0, pl.ds(z, TILE, stride=length), :].astype(bf16)


def quick_body(groups, ligand_grids, receptor_kernel):
    rotations, channels, depth, width, length = ligand_grids.shape
    pairs = channels // 2
    half = length // 2
    chips = groups // 2
    block = width // chips
    lot = depth * block
    chunks = half // SUB
    hops = groups // 4
    lasting = chunks - MOVED // SUB
    part = (lasting, rotations, half, TILE, length)
    rec = receptor_kernel[0]
    whole = pl.BlockSpec(memory_space=pltpu.VMEM)
    away = pl.BlockSpec(memory_space=pl.ANY)
    dma = pltpu.SemaphoreType.DMA
    best = pl.pallas_call(
        functools.partial(dock_kernel, groups, MOVED),
        out_shape=jax.ShapeDtypeStruct((length, half, length), bf16),
        in_specs=[whole] * 6 + [away] * 2,
        out_specs=whole,
        scratch_shapes=[
            pltpu.VMEM(ligand_grids.shape, f32),
            pltpu.VMEM((chips, rotations, pairs, 2, lot, length), bf16),
            pltpu.VMEM((pairs, groups, 2, lot, length), bf16),
            pltpu.VMEM((2, block * length, length), f32),
            pltpu.VMEM((half, pairs, 2 * block, length), bf16),
            pltpu.VMEM((groups, 2, half, pairs, 2 * block, length), bf16),
            pltpu.VMEM(rec.shape, bf16),
            pltpu.VMEM(part, bf16),
            pltpu.VMEM(part, bf16),
            pltpu.VMEM(part, bf16),
            pltpu.VMEM((2, SUB * rotations * length, length), f32),
            dma((pairs,)),
            dma((2,)),
            dma((pairs,)),
            dma((pairs, groups)),
            dma((pairs, groups)),
            dma((2, pairs)),
            dma((2, pairs)),
            dma((chunks,)),
            dma((chunks,)),
            dma((2, chunks, hops)),
            dma((2, chunks, hops)),
            dma((2, chunks, hops + 1)),
            dma((2, chunks, hops + 1)),
            dma((lasting, half // TILE)),
            dma((lasting, half // TILE)),
        ],
        compiler_params=pltpu.CompilerParams(
            collective_id=0, has_side_effects=True, vmem_limit_bytes=60 * 2**20
        ),
    )(*matrices(length, groups, MOVED), ligand_grids, rec)

    return best[None]


def choose(groups, slabs, ligand_grids, receptor_kernel):
    rotations, channels, depth, width, length = ligand_grids.shape
    fits = (
        slabs == 2
        and channels == 4
        and rotations == 2
        and depth == SUB
        and depth * groups == length
        and 2 * width == length
        and width // (groups // 2) == SUB
        and length % 128 == 0
        and (length // 2) % SUB == 0
        and groups == 4 * 4
        and (length // 2) % TILE == 0
    )
    if fits:
        return quick_body(groups, ligand_grids, receptor_kernel)
    return body(ligand_grids, receptor_kernel)


def solution(mesh):
    return jax.shard_map(
        functools.partial(choose, mesh.shape["grp"], mesh.shape["slab"]),
        mesh=mesh,
        in_specs=(P(None, None, "grp", "slab", None), P("grp", None, None, "slab", None, None)),
        out_specs=P("grp", None, "slab", None),
        check_vma=False,
    )
```

```python
import math

import functools

import jax
import jax.numpy as jnp
import numpy as np
from jax import lax
from jax.experimental import pallas as pl
from jax.experimental.pallas import tpu as pltpu
from jax.sharding import PartitionSpec as P

highest = lax.Precision.HIGHEST


def coefficients(length, inverse):
    positions = jnp.arange(length, dtype=jnp.int32)
    phases = positions[:, None] * positions[None, :] % length
    angles = phases.astype(jnp.float32) * (2.0 * math.pi / length)
    scaling = 1.0 / math.sqrt(length)
    cosine = jnp.cos(angles) * scaling
    sine_part = jnp.sin(angles) * scaling
    if inverse:
        sine_part = -sine_part
    upper_rows = jnp.stack([cosine, sine_part])
    lower_rows = jnp.stack([-sine_part, cosine])
    return jnp.stack([upper_rows, lower_rows])


def pack_pairs(ligand_piece):
    stacked = jnp.stack([ligand_piece[:, 0::2], ligand_piece[:, 1::2]])
    return stacked.reshape((2, stacked.shape[1] * stacked.shape[2]) + stacked.shape[3:])


def body(ligand_grids, receptor_kernel):
    length = ligand_grids.shape[4]
    rotations = ligand_grids.shape[0]
    channel_pairs = ligand_grids.shape[1] // 2
    forward = coefficients(length, False)
    forward_low = forward.astype(jnp.bfloat16)
    inverse_low = coefficients(length, True).astype(jnp.bfloat16)
    packed = pack_pairs(ligand_grids)
    lines = jnp.einsum("pqkn,qrzxn->pkrzx", forward, packed, precision=highest)
    columns = lax.all_to_all(
        lines.astype(jnp.bfloat16), "grp", split_axis=1, concat_axis=3, tiled=True
    ).astype(lines.dtype)
    partial_value = jnp.einsum("pqkn,qyrnx->pyrkx", forward, columns, precision=highest).astype(
        jnp.bfloat16
    )
    pieces = jnp.einsum(
        "pqkn,qyrzn->pyrzk",
        forward_low,
        lax.all_to_all(partial_value, "slab", split_axis=3, concat_axis=4, tiled=True),
        preferred_element_type=jnp.float32,
    ).astype(jnp.bfloat16)
    collected = lax.all_gather(pieces, "grp", axis=1, tiled=True)
    spectrum = jnp.transpose(collected, (0, 2, 3, 4, 1))
    spec_split = spectrum.reshape((2, rotations, channel_pairs) + spectrum.shape[2:])
    kernel_one = receptor_kernel[0]
    kernel_real = kernel_one[0][None].astype(jnp.float32)
    kernel_imag = kernel_one[1][None].astype(jnp.float32)
    spec_real = spec_split[0].astype(jnp.float32)
    spec_imag = spec_split[1].astype(jnp.float32)
    real_part = jnp.sum(kernel_real * spec_real - kernel_imag * spec_imag, axis=1)
    imag_part = jnp.sum(kernel_real * spec_imag + kernel_imag * spec_real, axis=1)
    product = jnp.stack([real_part, imag_part]).astype(jnp.bfloat16)
    rows_done = jnp.einsum(
        "pqkn,qrznm->przkm", inverse_low, product, preferred_element_type=jnp.float32
    ).astype(jnp.bfloat16)
    planes = jnp.einsum(
        "pqkn,qrzxn->przxk", inverse_low, rows_done, preferred_element_type=jnp.float32
    ).astype(jnp.bfloat16)
    scores = jnp.einsum(
        "qkn,qrnxy->rkxy",
        inverse_low[0],
        lax.all_to_all(planes, "slab", split_axis=3, concat_axis=2, tiled=True),
        preferred_element_type=jnp.float32,
    )
    return jnp.max(scores, axis=0).astype(jnp.bfloat16)[None]


TILE = 16
SUB = 8
MOVED = 8
f32 = jnp.float32
bf16 = jnp.bfloat16


def waves(length):
    positions = np.arange(length)
    angles = (positions[:, None] * positions[None, :] % length) * (2.0 * math.pi / length)
    scaling = 1.0 / math.sqrt(length)
    cosine, sine = np.cos(angles) * scaling, np.sin(angles) * scaling
    forward = np.stack([np.stack([cosine, sine]), np.stack([-sine, cosine])])
    inverse = np.stack([np.stack([cosine, -sine]), np.stack([sine, cosine])])
    return forward, inverse


def frequencies(length, moved, own):
    half = length // 2
    base, across = own * half, (1 - own) * half
    single = [base] + [base + n for n in range(moved + 1, half - moved)]
    kept = [base + half - moved + n for n in range(moved)]
    taken = [across + moved - n for n in range(moved)]
    return single, kept, taken


def matrices(length, groups, moved):
    forward, inverse = waves(length)
    half, side = length // 2, 2 * length
    chips = groups // 2
    orders, lasting = [], []
    for own in range(2):
        single, kept, taken = frequencies(length, moved, own)
        orders.append(single + [k for both in zip(kept, taken) for k in both])
        lasting.append(single + kept)
    fz, ix, mz = [], [], []
    for own in range(2):
        order = np.array(orders[own] + orders[1 - own])
        fz.append(forward[:, :, order].transpose(0, 2, 1, 3).reshape(side, side))
        order = (np.arange(length) + own * half) % length
        ix.append(inverse[:, :, order].transpose(0, 2, 1, 3).reshape(side, side))
        order = np.array(lasting[own] + lasting[1 - own])
        lines = inverse[0][:, :, order].reshape(2, length, len(order) // SUB, SUB)
        mz.append(lines.transpose(1, 2, 0, 3).reshape(length, 2 * len(order)))
    cells = forward.reshape(2, 2, length, 2, chips, half // chips)
    fx = cells.transpose(0, 2, 4, 3, 1, 5).reshape(side, side)
    fy = forward.transpose(1, 3, 0, 2).reshape(side, side)
    iy = inverse.transpose(1, 3, 0, 2).reshape(side, side)
    return [jnp.asarray(np.stack(m) if isinstance(m, list) else m).astype(bf16) for m in (fz, fy, fx, ix, iy, mz)]


def dot(a, b):
    return jnp.dot(a, b, preferred_element_type=f32)


def dock_kernel(
    groups, moved, fz_ref, fy_ref, fx_ref, ix_ref, iy_ref, mz_ref, lig_ref, rec_ref, out_ref,
    lig, blocks, lines, along, other, held, rec, mine, far, send, hold, tall,
    lig_sem, rec_sem, own_sem, line_out, line_in, give_out, give_in,
    swap_out, swap_in, ring_out, ring_in, pair_out, pair_in, slab_out, slab_in,
):
    me = lax.axis_index("grp")
    slab = lax.axis_index("slab")
    core = lax.rem(me, 2)
    chip = lax.div(me, 2)
    rotations, channels, depth, width, length = lig_ref.shape
    pairs = channels // 2
    chips = groups // 2
    block = width // chips
    lot = depth * block
    half = length // 2
    chunks = half // SUB
    single = (half - 2 * moved) // SUB
    lasting = single + moved // SUB
    steps = rotations * chunks
    height = groups // 4
    around = groups // 2
    row = lax.div(me, 4)
    column = lax.rem(chip, 2)
    spot = jnp.where(column == 0, row, around - 1 - row)
    far_step = around // 2 - 1
    MESH = pl.DeviceIdType.MESH

    def device(at, which):
        at = lax.rem(at + around, around)
        return jnp.where(at < height, at * 4, (around - 1 - at) * 4 + 2) + which

    def place(to):
        return {"grp": to, "slab": slab}

    def turned(by):
        return lax.rem(me + groups + by, groups)

    beside = (device(spot + 1, core), device(spot - 1, core))
    partner = device(spot, 1 - core)
    across = {"grp": me, "slab": 1 - slab}

    lig_loads = [
        pltpu.make_async_copy(lig_ref.at[r], lig.at[r], lig_sem.at[r]) for r in range(rotations)
    ]
    rest = half - 1 - moved
    rec_loads = [
        pltpu.make_async_copy(
            rec_ref.at[:, :, pl.ds(at, many)], rec.at[:, :, pl.ds(at, many)], rec_sem.at[n]
        )
        for n, (at, many) in enumerate([(0, 1), (moved + 1, rest)])
    ]
    for load in lig_loads:
        load.start()
    for load in rec_loads:
        load.start()

    barrier = pltpu.get_barrier_semaphore()
    pl.semaphore_signal(barrier, inc=1, device_id=across, device_id_type=MESH)

    @pl.loop(1, groups)
    def _(o):
        pl.semaphore_signal(barrier, inc=1, device_id=place(turned(o)), device_id_type=MESH)

    def give(p, j):
        at = pl.ds(1, moved)
        return pltpu.make_async_remote_copy(
            src_ref=rec_ref.at[p, j, at], dst_ref=rec.at[p, j, at],
            send_sem=give_out.at[p, j], recv_sem=give_in.at[p, j],
            device_id=across, device_id_type=MESH,
        )

    gives = [give(p, j) for p in range(2) for j in range(pairs)] if moved else []

    def line(o, r):
        to = turned(o)
        return pltpu.make_async_remote_copy(
            src_ref=blocks.at[lax.div(to, 2), lax.rem(to, 2), r], dst_ref=lines.at[r, me],
            send_sem=line_out.at[r, o], recv_sem=line_in.at[r, o],
            device_id=place(to), device_id_type=MESH,
        )

    def stay(r):
        return pltpu.make_async_copy(blocks.at[chip, core, r], lines.at[r, me], own_sem.at[r])

    for r in range(rotations):
        lig_loads[r].wait()

        @pl.loop(0, chips)
        def _(b):
            for j in range(pairs):
                for q in range(2):
                    piece = lig[r, 2 * j + q, :, pl.ds(pl.multiple_of(b * block, block), block), :]
                    blocks[b, j, r, q] = piece.reshape(lot, length).astype(bf16)

        if r == 0:
            pl.semaphore_wait(barrier, groups)

        @pl.loop(1, groups)
        def _(o):
            line(o, r).start()

        stay(r).start()
        if r == 0:
            for copy in gives[:pairs]:
                copy.start()

    def along_y(r, g):
        plane = dot(jnp.concatenate([lines[r, g, 0], lines[r, g, 1]], 1), fy_ref[...])
        for p in range(2):
            at = pl.ds(pl.multiple_of(g * lot, lot), lot)
            along[p, at, :] = plane[:, p * length : (p + 1) * length]

    def along_z():
        @pl.loop(0, block)
        def _(x):
            parts = [along[p, pl.ds(x, length, stride=block), :].astype(bf16) for p in range(2)]
            found = dot(fz_ref[slab], jnp.concatenate(parts, 0))
            for p in range(2):
                at = pl.ds(pl.multiple_of((p * block + x) * length, length), length)
                tall[at, :] = found[p * length : (p + 1) * length, :]

    def swap(c):
        at = pl.ds(c * SUB, SUB)
        return pltpu.make_async_remote_copy(
            src_ref=other.at[at], dst_ref=held.at[me, slab, at],
            send_sem=swap_out.at[c], recv_sem=swap_in.at[c],
            device_id=across, device_id_type=MESH,
        )

    def front(r):
        stay(r).wait()
        along_y(r, me)

        @pl.loop(1, groups)
        def _(o):
            line(o, r).wait_recv()
            along_y(r, turned(-o))

        along_z()

        @pl.loop(0, chunks)
        def _(c):
            @pl.loop(0, SUB, unroll=4)
            def _(n):
                k = c * SUB + n
                other[r * half + k] = tall[pl.ds(half + k, 2 * block, stride=length), :].astype(bf16)
                held[me, slab, r * half + k] = tall[pl.ds(k, 2 * block, stride=length), :].astype(bf16)

            swap(r * chunks + c).start()

    def origin(d, t):
        return spot - t if d == 0 else spot + t

    def part(slot, c, d, t):
        if t <= far_step:
            return held.at[slot, :, pl.ds(c * SUB, SUB)]
        return held.at[slot, :, pl.ds(c * SUB + d * (SUB // 2), SUB // 2)]

    def ring(d, c, t, slot):
        return pltpu.make_async_remote_copy(
            src_ref=part(slot, c, d, t + 1), dst_ref=part(slot, c, d, t + 1),
            send_sem=ring_out.at[d, c, t], recv_sem=ring_in.at[d, c, t],
            device_id=place(beside[d]), device_id_type=MESH,
        )

    def ring_send(d, c, t):
        ring(d, c, t, device(origin(d, t), core)).start()

    def ring_wait(d, c, t):
        ring(d, c, t, device(origin(d, t + 1), core)).wait_recv()

    def pair(d, c, t, which):
        slot = device(origin(d, t), which)
        return pltpu.make_async_remote_copy(
            src_ref=part(slot, c, d, t), dst_ref=part(slot, c, d, t),
            send_sem=pair_out.at[d, c, t], recv_sem=pair_in.at[d, c, t],
            device_id=place(partner), device_id_type=MESH,
        )

    def slab_copy(c, q):
        at = pl.ds(pl.multiple_of(q * TILE, TILE), TILE)
        return pltpu.make_async_remote_copy(
            src_ref=send.at[c, at], dst_ref=far.at[c, at],
            send_sem=slab_out.at[c, q], recv_sem=slab_in.at[c, q],
            device_id=across, device_id_type=MESH,
        )

    def open_chunk(c):
        swap(c).wait_recv()
        for d in range(2):
            ring_send(d, c, 0)
        pair(0, c, 0, core).start()

    def arrived(c, t):
        for d in range(2):
            ring_wait(d, c, t)
            if t < far_step:
                ring_send(d, c, t + 1)
            pair(d, c, t + 1, core).start()

    def product(z, slot):
        kr = [rec[0, j, slot].astype(f32) for j in range(pairs)]
        ki = [rec[1, j, slot].astype(f32) for j in range(pairs)]
        cols = [
            jnp.concatenate([held[2 * b + j, s, z] for b in range(chips) for s in range(2)], 0)
            for j in range(pairs)
        ]
        spec = dot(fx_ref[...], jnp.concatenate(cols, 1))
        sr = [spec[:length, j * length : (j + 1) * length] for j in range(pairs)]
        si = [spec[length:, j * length : (j + 1) * length] for j in range(pairs)]
        real = kr[0] * sr[0] - ki[0] * si[0] + (kr[1] * sr[1] - ki[1] * si[1])
        imag = kr[0] * si[0] + ki[0] * sr[0] + (kr[1] * si[1] + ki[1] * sr[1])
        return real.astype(bf16), imag.astype(bf16)

    def planes(both):
        parts = [product(z, slot) for z, slot in both]
        joined = jnp.concatenate([jnp.concatenate([part[p] for part in parts], 1) for p in range(2)], 0)
        done = dot(ix_ref[slab], joined).astype(bf16)
        flat = []
        for n in range(len(both)):
            at = slice(n * length, (n + 1) * length)
            flat.append(jnp.concatenate([done[:length, at], done[length:, at]], 1))
        return dot(jnp.concatenate(flat, 0), iy_ref[...])

    def compute(s):
        c = lax.rem(s, chunks)

        @pl.when(c < single)
        def _():
            @pl.loop(0, SUB // 2, unroll=2)
            def _(n):
                both = []
                for k in (2 * n, 2 * n + 1):
                    z = c * SUB + k
                    both.append((s * SUB + k, jnp.where(z == 0, 0, z + moved)))
                found = planes(both)
                for p in range(2):
                    at = pl.ds(pl.multiple_of(2 * n * length, 2 * length), 2 * length)
                    hold[p, at, :] = found[:, p * length : (p + 1) * length]

        if moved:
            @pl.when(c >= single)
            def _():
                @pl.loop(0, SUB // 2)
                def _(n):
                    z = s * SUB + 2 * n
                    m = (c - single) * (SUB // 2) + n
                    found = planes([(z, half - moved + m), (z + 1, moved - m)])
                    one, two = found[:length], found[length:]
                    at = pl.ds(pl.multiple_of(lax.rem(m, SUB) * length, length), length)
                    hold[0, at, :] = one[:, :length] + two[:, :length]
                    hold[1, at, :] = one[:, length:] - two[:, length:]

    def collect(t, ref, first):
        @pl.loop(0, half, unroll=4)
        def _(x):
            at = pl.ds(first + x, SUB, stride=length)
            ref[t, x] = jnp.concatenate([hold[0, at, :], hold[1, at, :]], 0).astype(bf16)

    def hand_over(s):
        r, c = lax.div(s, chunks), lax.rem(s, chunks)
        over = c - single

        @pl.when((over < 0) | (lax.rem(jnp.maximum(over, 0), 2) == 1))
        def _():
            t = r * lasting + jnp.where(over < 0, c, single + lax.div(jnp.maximum(over, 0), 2))
            collect(t, send, half)
            for q in range(half // TILE):
                slab_copy(t, q).start()
            collect(t, mine, 0)

    def score(r, q):
        @pl.loop(r * lasting, (r + 1) * lasting)
        def _(t):
            slab_copy(t, q).wait_send()
            slab_copy(t, q).wait_recv()

        @pl.loop(0, TILE // 2, unroll=2)
        def _(n):
            cols = []
            for x in (2 * n, 2 * n + 1):
                tiles = [ref[r * lasting + t, q * TILE + x] for ref in (mine, far) for t in range(lasting)]
                cols.append(jnp.concatenate(tiles, 0))
            found = dot(mz_ref[slab], jnp.concatenate(cols, 1))
            for x in range(2):
                at = pl.ds(pl.multiple_of((2 * n + x) * length, length), length)
                tall[at, :] = found[:, x * length : (x + 1) * length]

        @pl.loop(0, length, unroll=4)
        def _(z):
            at = pl.ds(pl.multiple_of(q * TILE, TILE), TILE)
            best = tall[pl.ds(z, TILE, stride=length), :]
            if r > 0:
                best = jnp.maximum(out_ref[z, at, :].astype(f32), best)
            out_ref[z, at, :] = best.astype(bf16)

    front(0)
    for copy in gives[pairs:]:
        copy.start()
    open_chunk(0)
    early = half // TILE
    begin = steps + far_step - early - 2

    @pl.loop(0, steps + far_step)
    def _(i):
        @pl.when(i + 1 < steps)
        def _():
            open_chunk(i + 1)

        for t in range(far_step - 1, -1, -1):
            @pl.when((i >= t) & (i - t < steps))
            def _():
                arrived(i - t, t)

        @pl.when(i == far_step)
        def _():
            for load in rec_loads:
                load.wait()

        if moved:
            @pl.when(i == far_step + single)
            def _():
                for copy in gives:
                    copy.wait()

        @pl.when(i >= far_step)
        def _():
            s = i - far_step
            arrived(s, far_step)
            pair(0, s, 0, 1 - core).wait_recv()
            for t in range(1, far_step + 2):
                for d in range(2):
                    pair(d, s, t, 1 - core).wait_recv()
            compute(s)
            hand_over(s)

        @pl.when(i == far_step)
        def _():
            front(1)

        @pl.when((i >= begin) & (i < begin + early))
        def _():
            score(0, i - begin)

    for r in range(rotations):
        @pl.loop(1, groups)
        def _(o):
            line(o, r).wait_send()

    @pl.loop(0, steps)
    def _(s):
        for t in range(far_step + 1):
            for d in range(2):
                ring(d, s, t, device(origin(d, t), core)).wait_send()
                pair(d, s, t + 1, core).wait_send()
        pair(0, s, 0, core).wait_send()
        swap(s).wait_send()

    @pl.loop(0, half // TILE)
    def _(q):
        score(1, q)


def quick_body(groups, ligand_grids, receptor_kernel):
    rotations, channels, depth, width, length = ligand_grids.shape
    pairs = channels // 2
    half = length // 2
    chips = groups // 2
    block = width // chips
    lot = depth * block
    chunks = half // SUB
    hops = groups // 4
    lasting = chunks - MOVED // SUB
    steps = rotations * chunks
    part = (rotations * lasting, half, TILE, length)
    rec = receptor_kernel[0]
    whole = pl.BlockSpec(memory_space=pltpu.VMEM)
    away = pl.BlockSpec(memory_space=pl.ANY)
    dma = pltpu.SemaphoreType.DMA
    best = pl.pallas_call(
        functools.partial(dock_kernel, groups, MOVED),
        out_shape=jax.ShapeDtypeStruct((length, half, length), bf16),
        in_specs=[whole] * 6 + [away] * 2,
        out_specs=whole,
        scratch_shapes=[
            pltpu.VMEM(ligand_grids.shape, f32),
            pltpu.VMEM((chips, pairs, rotations, 2, lot, length), bf16),
            pltpu.VMEM((rotations, groups, 2, lot, length), bf16),
            pltpu.VMEM((2, block * length, length), f32),
            pltpu.VMEM((rotations * half, 2 * block, length), bf16),
            pltpu.VMEM((groups, 2, rotations * half, 2 * block, length), bf16),
            pltpu.VMEM(rec.shape, bf16),
            pltpu.VMEM(part, bf16),
            pltpu.VMEM(part, bf16),
            pltpu.VMEM(part, bf16),
            pltpu.VMEM((2, SUB * length, length), f32),
            pltpu.VMEM((TILE * length, length), f32),
            dma((rotations,)),
            dma((2,)),
            dma((rotations,)),
            dma((rotations, groups)),
            dma((rotations, groups)),
            dma((2, pairs)),
            dma((2, pairs)),
            dma((steps,)),
            dma((steps,)),
            dma((2, steps, hops)),
            dma((2, steps, hops)),
            dma((2, steps, hops + 1)),
            dma((2, steps, hops + 1)),
            dma((rotations * lasting, half // TILE)),
            dma((rotations * lasting, half // TILE)),
        ],
        compiler_params=pltpu.CompilerParams(
            collective_id=0, has_side_effects=True, vmem_limit_bytes=60 * 2**20
        ),
    )(*matrices(length, groups, MOVED), ligand_grids, rec)

    return best[None]


def choose(groups, slabs, ligand_grids, receptor_kernel):
    rotations, channels, depth, width, length = ligand_grids.shape
    fits = (
        slabs == 2
        and channels == 4
        and rotations == 2
        and depth == SUB
        and depth * groups == length
        and 2 * width == length
        and width // (groups // 2) == SUB
        and length % 128 == 0
        and (length // 2) % SUB == 0
        and groups == 4 * 4
        and (length // 2) % TILE == 0
    )
    if fits:
        return quick_body(groups, ligand_grids, receptor_kernel)
    return body(ligand_grids, receptor_kernel)


def solution(mesh):
    return jax.shard_map(
        functools.partial(choose, mesh.shape["grp"], mesh.shape["slab"]),
        mesh=mesh,
        in_specs=(P(None, None, "grp", "slab", None), P("grp", None, None, "slab", None, None)),
        out_specs=P("grp", None, "slab", None),
        check_vma=False,
    )
```

```python
import math

import functools

import jax
import jax.numpy as jnp
import numpy as np
from jax import lax
from jax.experimental import pallas as pl
from jax.experimental.pallas import tpu as pltpu
from jax.sharding import PartitionSpec as P

highest = lax.Precision.HIGHEST


def coefficients(length, inverse):
    positions = jnp.arange(length, dtype=jnp.int32)
    phases = positions[:, None] * positions[None, :] % length
    angles = phases.astype(jnp.float32) * (2.0 * math.pi / length)
    scaling = 1.0 / math.sqrt(length)
    cosine = jnp.cos(angles) * scaling
    sine_part = jnp.sin(angles) * scaling
    if inverse:
        sine_part = -sine_part
    upper_rows = jnp.stack([cosine, sine_part])
    lower_rows = jnp.stack([-sine_part, cosine])
    return jnp.stack([upper_rows, lower_rows])


def pack_pairs(ligand_piece):
    stacked = jnp.stack([ligand_piece[:, 0::2], ligand_piece[:, 1::2]])
    return stacked.reshape((2, stacked.shape[1] * stacked.shape[2]) + stacked.shape[3:])


def body(ligand_grids, receptor_kernel):
    length = ligand_grids.shape[4]
    rotations = ligand_grids.shape[0]
    channel_pairs = ligand_grids.shape[1] // 2
    forward = coefficients(length, False)
    forward_low = forward.astype(jnp.bfloat16)
    inverse_low = coefficients(length, True).astype(jnp.bfloat16)
    packed = pack_pairs(ligand_grids)
    lines = jnp.einsum("pqkn,qrzxn->pkrzx", forward, packed, precision=highest)
    columns = lax.all_to_all(
        lines.astype(jnp.bfloat16), "grp", split_axis=1, concat_axis=3, tiled=True
    ).astype(lines.dtype)
    partial_value = jnp.einsum("pqkn,qyrnx->pyrkx", forward, columns, precision=highest).astype(
        jnp.bfloat16
    )
    pieces = jnp.einsum(
        "pqkn,qyrzn->pyrzk",
        forward_low,
        lax.all_to_all(partial_value, "slab", split_axis=3, concat_axis=4, tiled=True),
        preferred_element_type=jnp.float32,
    ).astype(jnp.bfloat16)
    collected = lax.all_gather(pieces, "grp", axis=1, tiled=True)
    spectrum = jnp.transpose(collected, (0, 2, 3, 4, 1))
    spec_split = spectrum.reshape((2, rotations, channel_pairs) + spectrum.shape[2:])
    kernel_one = receptor_kernel[0]
    kernel_real = kernel_one[0][None].astype(jnp.float32)
    kernel_imag = kernel_one[1][None].astype(jnp.float32)
    spec_real = spec_split[0].astype(jnp.float32)
    spec_imag = spec_split[1].astype(jnp.float32)
    real_part = jnp.sum(kernel_real * spec_real - kernel_imag * spec_imag, axis=1)
    imag_part = jnp.sum(kernel_real * spec_imag + kernel_imag * spec_real, axis=1)
    product = jnp.stack([real_part, imag_part]).astype(jnp.bfloat16)
    rows_done = jnp.einsum(
        "pqkn,qrznm->przkm", inverse_low, product, preferred_element_type=jnp.float32
    ).astype(jnp.bfloat16)
    planes = jnp.einsum(
        "pqkn,qrzxn->przxk", inverse_low, rows_done, preferred_element_type=jnp.float32
    ).astype(jnp.bfloat16)
    scores = jnp.einsum(
        "qkn,qrnxy->rkxy",
        inverse_low[0],
        lax.all_to_all(planes, "slab", split_axis=3, concat_axis=2, tiled=True),
        preferred_element_type=jnp.float32,
    )
    return jnp.max(scores, axis=0).astype(jnp.bfloat16)[None]


TILE = 16
SUB = 8
MOVED = 16
AHEAD = 1
f32 = jnp.float32
bf16 = jnp.bfloat16


def waves(length):
    positions = np.arange(length)
    angles = (positions[:, None] * positions[None, :] % length) * (2.0 * math.pi / length)
    scaling = 1.0 / math.sqrt(length)
    cosine, sine = np.cos(angles) * scaling, np.sin(angles) * scaling
    forward = np.stack([np.stack([cosine, sine]), np.stack([-sine, cosine])])
    inverse = np.stack([np.stack([cosine, -sine]), np.stack([sine, cosine])])
    return forward, inverse


def frequencies(length, moved, own):
    half = length // 2
    base, across = own * half, (1 - own) * half
    single = [base] + [base + n for n in range(moved + 1, half - moved)]
    kept = [base + half - moved + n for n in range(moved)]
    taken = [across + moved - n for n in range(moved)]
    return single, kept, taken


def matrices(length, groups, moved):
    forward, inverse = waves(length)
    half, side = length // 2, 2 * length
    chips = groups // 2
    orders, lasting = [], []
    for own in range(2):
        single, kept, taken = frequencies(length, moved, own)
        orders.append(single + [k for both in zip(kept, taken) for k in both])
        lasting.append(single + kept)
    fz, ix, mz = [], [], []
    for own in range(2):
        order = np.array(orders[own] + orders[1 - own])
        fz.append(forward[:, :, order].transpose(0, 2, 1, 3).reshape(side, side))
        order = (np.arange(length) + own * half) % length
        ix.append(inverse[:, :, order].transpose(0, 2, 1, 3).reshape(side, side))
        order = np.array(lasting[own] + lasting[1 - own])
        lines = inverse[0][:, :, order].reshape(2, length, len(order) // SUB, SUB)
        mz.append(lines.transpose(1, 2, 0, 3).reshape(length, 2 * len(order)))
    cells = forward.reshape(2, 2, length, 2, chips, half // chips)
    fx = cells.transpose(0, 2, 4, 3, 1, 5).reshape(side, side)
    fy = forward.transpose(1, 3, 0, 2).reshape(side, side)
    iy = inverse.transpose(1, 3, 0, 2).reshape(side, side)
    return [jnp.asarray(np.stack(m) if isinstance(m, list) else m).astype(bf16) for m in (fz, fy, fx, ix, iy, mz)]


def dot(a, b):
    return jnp.dot(a, b, preferred_element_type=f32)


def dock_kernel(
    groups, moved, fz_ref, fy_ref, fx_ref, ix_ref, iy_ref, mz_ref, lig_ref, rec_ref, out_ref,
    lig, blocks, lines, along, other, held, rec, mine, far, send, hold,
    lig_sem, rec_sem, own_sem, line_out, line_in, give_out, give_in,
    swap_out, swap_in, ring_out, ring_in, pair_out, pair_in, slab_out, slab_in,
):
    me = lax.axis_index("grp")
    slab = lax.axis_index("slab")
    core = lax.rem(me, 2)
    chip = lax.div(me, 2)
    rotations, channels, depth, width, length = lig_ref.shape
    pairs = channels // 2
    chips = groups // 2
    block = width // chips
    lot = depth * block
    half = length // 2
    chunks = half // SUB
    single = (half - 2 * moved) // SUB
    lasting = single + moved // SUB
    rows = rotations * length
    height = groups // 4
    around = groups // 2
    row = lax.div(me, 4)
    column = lax.rem(chip, 2)
    spot = jnp.where(column == 0, row, around - 1 - row)
    far_step = around // 2 - 1
    MESH = pl.DeviceIdType.MESH

    def device(at, which):
        at = lax.rem(at + around, around)
        return jnp.where(at < height, at * 4, (around - 1 - at) * 4 + 2) + which

    def place(to):
        return {"grp": to, "slab": slab}

    def turned(by):
        return lax.rem(me + groups + by, groups)

    beside = (device(spot + 1, core), device(spot - 1, core))
    partner = device(spot, 1 - core)
    across = {"grp": me, "slab": 1 - slab}

    lig_loads = [
        pltpu.make_async_copy(lig_ref.at[:, pl.ds(2 * j, 2)], lig.at[:, pl.ds(2 * j, 2)], lig_sem.at[j])
        for j in range(pairs)
    ]
    rest = half - 1 - moved
    rec_loads = [
        pltpu.make_async_copy(
            rec_ref.at[:, :, pl.ds(at, many)], rec.at[:, :, pl.ds(at, many)], rec_sem.at[n]
        )
        for n, (at, many) in enumerate([(0, 1), (moved + 1, rest)])
    ]
    for load in lig_loads:
        load.start()
    for load in rec_loads:
        load.start()

    barrier = pltpu.get_barrier_semaphore()
    pl.semaphore_signal(barrier, inc=1, device_id=across, device_id_type=MESH)

    @pl.loop(1, groups)
    def _(o):
        pl.semaphore_signal(barrier, inc=1, device_id=place(turned(o)), device_id_type=MESH)

    def give(p, j):
        at = pl.ds(1, moved)
        return pltpu.make_async_remote_copy(
            src_ref=rec_ref.at[p, j, at], dst_ref=rec.at[p, j, at],
            send_sem=give_out.at[p, j], recv_sem=give_in.at[p, j],
            device_id=across, device_id_type=MESH,
        )

    gives = [give(p, j) for p in range(2) for j in range(pairs)] if moved else []

    def line(o, j):
        to = turned(o)
        return pltpu.make_async_remote_copy(
            src_ref=blocks.at[lax.div(to, 2), lax.rem(to, 2), j], dst_ref=lines.at[j, me],
            send_sem=line_out.at[j, o], recv_sem=line_in.at[j, o],
            device_id=place(to), device_id_type=MESH,
        )

    def stay(j):
        return pltpu.make_async_copy(blocks.at[chip, core, j], lines.at[j, me], own_sem.at[j])

    for j in range(pairs):
        lig_loads[j].wait()

        @pl.loop(0, chips)
        def _(b):
            for r in range(rotations):
                for q in range(2):
                    piece = lig[r, 2 * j + q, :, pl.ds(pl.multiple_of(b * block, block), block), :]
                    blocks[b, r, j, q] = piece.reshape(lot, length).astype(bf16)

        if j == 0:
            pl.semaphore_wait(barrier, groups)

        @pl.loop(1, groups)
        def _(o):
            line(o, j).start()

        stay(j).start()
    for copy in gives[:pairs]:
        copy.start()

    def along_y(j, g):
        plane = dot(jnp.concatenate([lines[j, g, 0], lines[j, g, 1]], 1), fy_ref[...])
        for p in range(2):
            at = pl.ds(pl.multiple_of(g * lot, lot), lot)
            along[p, at, :] = plane[:, p * length : (p + 1) * length]

    def along_z():
        @pl.loop(0, block)
        def _(x):
            parts = [along[p, pl.ds(x, length, stride=block), :].astype(bf16) for p in range(2)]
            found = dot(fz_ref[slab], jnp.concatenate(parts, 0))
            for p in range(2):
                at = pl.ds(pl.multiple_of((p * block + x) * length, length), length)
                hold[0, at, :] = found[p * length : (p + 1) * length, :]

    def swap(c):
        at = pl.ds(c * SUB, SUB)
        return pltpu.make_async_remote_copy(
            src_ref=other.at[at], dst_ref=held.at[me, slab, at],
            send_sem=swap_out.at[c], recv_sem=swap_in.at[c],
            device_id=across, device_id_type=MESH,
        )

    for j in range(pairs):
        stay(j).wait()
        along_y(j, me)

        @pl.loop(1, groups)
        def _(o):
            line(o, j).wait_recv()
            along_y(j, turned(-o))

        along_z()

        @pl.loop(0, chunks)
        def _(c):
            @pl.loop(0, SUB, unroll=4)
            def _(n):
                k = c * SUB + n
                other[k, j] = hold[0, pl.ds(half + k, 2 * block, stride=length), :].astype(bf16)
                held[me, slab, k, j] = hold[0, pl.ds(k, 2 * block, stride=length), :].astype(bf16)

            if j == pairs - 1:
                swap(c).start()

    def origin(d, t):
        return spot - t if d == 0 else spot + t

    def part(slot, c, d, t):
        if t <= far_step:
            return held.at[slot, :, pl.ds(c * SUB, SUB)]
        return held.at[slot, :, pl.ds(c * SUB + d * (SUB // 2), SUB // 2)]

    def ring(d, c, t, slot):
        return pltpu.make_async_remote_copy(
            src_ref=part(slot, c, d, t + 1), dst_ref=part(slot, c, d, t + 1),
            send_sem=ring_out.at[d, c, t], recv_sem=ring_in.at[d, c, t],
            device_id=place(beside[d]), device_id_type=MESH,
        )

    def ring_send(d, c, t):
        ring(d, c, t, device(origin(d, t), core)).start()

    def ring_wait(d, c, t):
        ring(d, c, t, device(origin(d, t + 1), core)).wait_recv()

    def pair(d, c, t, which):
        slot = device(origin(d, t), which)
        return pltpu.make_async_remote_copy(
            src_ref=part(slot, c, d, t), dst_ref=part(slot, c, d, t),
            send_sem=pair_out.at[d, c, t], recv_sem=pair_in.at[d, c, t],
            device_id=place(partner), device_id_type=MESH,
        )

    def slab_copy(c, q):
        at = pl.ds(pl.multiple_of(q * TILE, TILE), TILE)
        return pltpu.make_async_remote_copy(
            src_ref=send.at[c, :, at], dst_ref=far.at[c, :, at],
            send_sem=slab_out.at[c, q], recv_sem=slab_in.at[c, q],
            device_id=across, device_id_type=MESH,
        )

    def slab_whole(c):
        return pltpu.make_async_remote_copy(
            src_ref=send.at[c], dst_ref=far.at[c],
            send_sem=slab_out.at[c, 0], recv_sem=slab_in.at[c, 0],
            device_id=across, device_id_type=MESH,
        )

    def open_chunk(c):
        swap(c).wait_recv()
        for d in range(2):
            ring_send(d, c, 0)
        pair(0, c, 0, core).start()

    def arrived(c, t):
        for d in range(2):
            ring_wait(d, c, t)
            if t < far_step:
                ring_send(d, c, t + 1)
            pair(d, c, t + 1, core).start()

    def plane(z, slot):
        kr = [rec[0, j, slot].astype(f32) for j in range(pairs)]
        ki = [rec[1, j, slot].astype(f32) for j in range(pairs)]
        real, imag = [], []
        for r in range(rotations):
            cols = [
                jnp.concatenate([held[2 * b + r, s, z, j] for b in range(chips) for s in range(2)], 0)
                for j in range(pairs)
            ]
            spec = dot(fx_ref[...], jnp.concatenate(cols, 1))
            sr = [spec[:length, j * length : (j + 1) * length] for j in range(pairs)]
            si = [spec[length:, j * length : (j + 1) * length] for j in range(pairs)]
            real.append(kr[0] * sr[0] - ki[0] * si[0] + (kr[1] * sr[1] - ki[1] * si[1]))
            imag.append(kr[0] * si[0] + ki[0] * sr[0] + (kr[1] * si[1] + ki[1] * sr[1]))
        product = jnp.concatenate(
            [jnp.concatenate(real, 1).astype(bf16), jnp.concatenate(imag, 1).astype(bf16)], 0
        )
        done = dot(ix_ref[slab], product).astype(bf16)
        flat = []
        for r in range(rotations):
            at = slice(r * length, (r + 1) * length)
            flat.append(jnp.concatenate([done[:length, at], done[length:, at]], 1))
        return dot(jnp.concatenate(flat, 0), iy_ref[...])

    def keep(k, parts):
        for p in range(2):
            hold[p, pl.ds(pl.multiple_of(k * rows, rows), rows), :] = parts[p]

    def alone(c, first):
        @pl.loop(first, first + SUB // 2, unroll=2)
        def _(k):
            z = c * SUB + k
            both = plane(z, jnp.where(z == 0, 0, z + moved))
            keep(k, [both[:, :length], both[:, length:]])

    def mirrored(c, first):
        @pl.loop(0, SUB // 4)
        def _(q):
            z = c * SUB + first + 2 * q
            n = lax.div(z - single * SUB, 2)
            one = plane(z, half - moved + n)
            two = plane(z + 1, moved - n)
            keep(lax.rem(n, SUB), [one[:, :length] + two[:, :length], one[:, length:] - two[:, length:]])

    def compute(c, first):
        @pl.when(c < single)
        def _():
            alone(c, first)

        if moved:
            @pl.when(c >= single)
            def _():
                mirrored(c, first)

    def collect(c, ref, first):
        @pl.loop(0, half, unroll=4)
        def _(x):
            for r in range(rotations):
                at = pl.ds(r * length + first + x, SUB, stride=rows)
                ref[c, r, x] = jnp.concatenate([hold[0, at, :], hold[1, at, :]], 0).astype(bf16)

    for copy in gives[pairs:]:
        copy.start()
    for c in range(AHEAD):
        open_chunk(c)

    @pl.loop(0, chunks + 2)
    def _(i):
        c1, c2 = i - 1, i - 2

        @pl.when((c1 >= 0) & (c1 < chunks))
        def _():
            arrived(c1, 1)

        @pl.when(i == 2)
        def _():
            for load in rec_loads:
                load.wait()

        if moved:
            @pl.when(i == 2 + single)
            def _():
                for copy in gives:
                    copy.wait()

        @pl.when(c2 >= 0)
        def _():
            arrived(c2, far_step)
            pair(0, c2, 0, 1 - core).wait_recv()
            for t in range(1, far_step + 2):
                for d in range(2):
                    pair(d, c2, t, 1 - core).wait_recv()
            compute(c2, 0)

        @pl.when(i < chunks)
        def _():
            arrived(i, 0)

        @pl.when((c1 >= 0) & (c1 < chunks))
        def _():
            arrived(c1, 2)

        @pl.when(i + AHEAD < chunks)
        def _():
            open_chunk(i + AHEAD)

        @pl.when(c2 >= 0)
        def _():
            compute(c2, SUB // 2)
            over = c2 - single

            @pl.when((over < 0) | (lax.rem(jnp.maximum(over, 0), 2) == 1))
            def _():
                c = jnp.where(over < 0, c2, single + lax.div(jnp.maximum(over, 0), 2))
                collect(c, send, half)

                @pl.when(c < lasting - 1)
                def _():
                    slab_whole(c).start()

                @pl.when(c == lasting - 1)
                def _():
                    for q in range(half // TILE):
                        slab_copy(lasting - 1, q).start()

                collect(c, mine, 0)

    for j in range(pairs):
        @pl.loop(1, groups)
        def _(o):
            line(o, j).wait_send()

    @pl.loop(0, chunks)
    def _(c):
        for t in range(far_step + 1):
            for d in range(2):
                ring(d, c, t, device(origin(d, t), core)).wait_send()
                pair(d, c, t + 1, core).wait_send()
        pair(0, c, 0, core).wait_send()
        swap(c).wait_send()

    @pl.loop(0, half // TILE)
    def _(q):
        @pl.when(q == 0)
        def _():
            @pl.loop(0, lasting - 1)
            def _(c):
                slab_whole(c).wait_send()
                slab_whole(c).wait_recv()

        slab_copy(lasting - 1, q).wait_send()
        slab_copy(lasting - 1, q).wait_recv()

        @pl.loop(0, TILE, unroll=2)
        def _(x):
            cols = []
            for r in range(rotations):
                tiles = [ref[t, r, q * TILE + x] for ref in (mine, far) for t in range(lasting)]
                cols.append(jnp.concatenate(tiles, 0))
            scores = dot(mz_ref[slab], jnp.concatenate(cols, 1))
            best = scores[:, :length]
            for r in range(1, rotations):
                best = jnp.maximum(best, scores[:, r * length : (r + 1) * length])
            hold[0, pl.ds(x * length, length), :] = best

        @pl.loop(0, length, unroll=4)
        def _(z):
            at = pl.ds(pl.multiple_of(q * TILE, TILE), TILE)
            out_ref[z, at, :] = hold[0, pl.ds(z, TILE, stride=length), :].astype(bf16)


def quick_body(groups, ligand_grids, receptor_kernel):
    rotations, channels, depth, width, length = ligand_grids.shape
    pairs = channels // 2
    half = length // 2
    chips = groups // 2
    block = width // chips
    lot = depth * block
    chunks = half // SUB
    hops = groups // 4
    lasting = chunks - MOVED // SUB
    part = (lasting, rotations, half, TILE, length)
    rec = receptor_kernel[0]
    whole = pl.BlockSpec(memory_space=pltpu.VMEM)
    away = pl.BlockSpec(memory_space=pl.ANY)
    dma = pltpu.SemaphoreType.DMA
    best = pl.pallas_call(
        functools.partial(dock_kernel, groups, MOVED),
        out_shape=jax.ShapeDtypeStruct((length, half, length), bf16),
        in_specs=[whole] * 6 + [away] * 2,
        out_specs=whole,
        scratch_shapes=[
            pltpu.VMEM(ligand_grids.shape, f32),
            pltpu.VMEM((chips, rotations, pairs, 2, lot, length), bf16),
            pltpu.VMEM((pairs, groups, 2, lot, length), bf16),
            pltpu.VMEM((2, block * length, length), f32),
            pltpu.VMEM((half, pairs, 2 * block, length), bf16),
            pltpu.VMEM((groups, 2, half, pairs, 2 * block, length), bf16),
            pltpu.VMEM(rec.shape, bf16),
            pltpu.VMEM(part, bf16),
            pltpu.VMEM(part, bf16),
            pltpu.VMEM(part, bf16),
            pltpu.VMEM((2, SUB * rotations * length, length), f32),
            dma((pairs,)),
            dma((2,)),
            dma((pairs,)),
            dma((pairs, groups)),
            dma((pairs, groups)),
            dma((2, pairs)),
            dma((2, pairs)),
            dma((chunks,)),
            dma((chunks,)),
            dma((2, chunks, hops)),
            dma((2, chunks, hops)),
            dma((2, chunks, hops + 1)),
            dma((2, chunks, hops + 1)),
            dma((lasting, half // TILE)),
            dma((lasting, half // TILE)),
        ],
        compiler_params=pltpu.CompilerParams(
            collective_id=0, has_side_effects=True, vmem_limit_bytes=60 * 2**20
        ),
    )(*matrices(length, groups, MOVED), ligand_grids, rec)

    return best[None]


def choose(groups, slabs, ligand_grids, receptor_kernel):
    rotations, channels, depth, width, length = ligand_grids.shape
    fits = (
        slabs == 2
        and channels == 4
        and rotations == 2
        and depth == SUB
        and depth * groups == length
        and 2 * width == length
        and width // (groups // 2) == SUB
        and length % 128 == 0
        and (length // 2) % SUB == 0
        and groups == 4 * 4
        and (length // 2) % TILE == 0
    )
    if fits:
        return quick_body(groups, ligand_grids, receptor_kernel)
    return body(ligand_grids, receptor_kernel)


def solution(mesh):
    return jax.shard_map(
        functools.partial(choose, mesh.shape["grp"], mesh.shape["slab"]),
        mesh=mesh,
        in_specs=(P(None, None, "grp", "slab", None), P("grp", None, None, "slab", None, None)),
        out_specs=P("grp", None, "slab", None),
        check_vma=False,
    )
```
